32 devices in a mesh: rows: 8 (over z, core), feat: 4 (over y, x).
Axes of the slice: x: 2, y: 2, z: 4, core: 2. Of those that a mesh axis runs over, the one named last changes fastest.
Arguments:
- features: float32 [8192, 2048], P('rows', 'feat'), may hold values from -200 to 200
- targets: float32 [8192, 2048], P('rows', 'feat'), may hold values from -2000 to 2000
Outputs:
- coefficients: float32 [2048, 2048], P('feat')
- residual: float32 [8192, 2048], P('rows', 'feat')
The draws below stay inside these ranges and needn't reach their ends.
All inputs are finite; a program needn't handle non-finite values.
Results may differ from the reference program's by a relative error of at most 0.0003.
Values sent between devices are 32-bit elements; how exact they have to be, the bound alone decides.
A program may use at most 64 MiB of HBM per device.

```python
import jax
import jax.numpy as jnp
from jax import lax

B = 512
TGT = 2048
SWEEPS = 1
NBLK = 4
ROWS = 8192
FEATS = 2048
TG = 512


def joint_draw(key):
    k_mix = jax.random.fold_in(key, 11)
    k_col = jax.random.fold_in(key, 12)
    k_true = jax.random.fold_in(key, 14)
    k_noise = jax.random.fold_in(key, 15)
    base = jax.random.normal(k_mix, (ROWS, FEATS), jnp.float32)
    mixed = base + 0.7 * jnp.roll(base, -(B // 2), axis=1)
    col_scale = jnp.exp(jax.random.uniform(k_col, (FEATS,), jnp.float32, 0.0, jnp.log(4.0)))
    data = jnp.clip(mixed * col_scale[None, :], -200.0, 200.0)
    truth = 0.1 * jax.random.normal(k_true, (FEATS, TGT), jnp.float32)
    noise = jax.random.normal(k_noise, (ROWS, TGT), jnp.float32)
    rhs = jnp.dot(data, truth, precision=lax.Precision.HIGHEST) + noise
    return (data, jnp.clip(rhs, -2000.0, 2000.0))


def draw_features(key, part):
    return joint_draw(key)[0]


def draw_targets(key, part):
    return joint_draw(key)[1]


def setup_inputs(seed: int = 0) -> dict:
    key_list = jax.random.split(jax.random.key(seed), 3)
    return {
        "features": draw_features(jax.random.fold_in(key_list[2], 71), 0),
        "targets": draw_targets(jax.random.fold_in(key_list[2], 71), 0),
    }


def reference(features, targets):
    hi = lax.Precision.HIGHEST

    def block_factor(j):
        block = lax.dynamic_slice_in_dim(features, j * B, B, 1)
        gram = lax.dot_general(block.astype(jnp.float32), block.astype(jnp.float32), (((0,), (0,)), ((), ())), precision=hi, preferred_element_type=jnp.float32)
        return jnp.linalg.cholesky(gram)
    lowers = lax.map(block_factor, jnp.arange(NBLK, dtype=jnp.int32))

    def one_group(group):
        start_res = lax.dynamic_slice_in_dim(targets, group * TG, TG, 1)
        coef = jnp.zeros((FEATS, TG), jnp.float32)

        def section(s, carry):
            coef, res = carry
            j = ((group + s) % NBLK).astype(jnp.int32)
            block = lax.dynamic_slice_in_dim(features, j * B, B, 1)
            product = lax.dot_general(block.astype(jnp.float32), res.astype(jnp.float32), (((0,), (0,)), ((), ())), precision=hi, preferred_element_type=jnp.float32)
            lower = lowers[j]
            step = jax.scipy.linalg.cho_solve((lower, True), product)
            old = lax.dynamic_slice_in_dim(coef, j * B, B, 0)
            coef = lax.dynamic_update_slice_in_dim(coef, old + step, j * B, 0)
            res = res - jnp.dot(block.astype(jnp.float32), step.astype(jnp.float32), precision=hi, preferred_element_type=jnp.float32)
            return (coef, res)
        return lax.fori_loop(0, SWEEPS * NBLK, section, (coef, start_res))
    coefs, residuals = lax.map(one_group, jnp.arange(NBLK, dtype=jnp.int32))
    coefficients = jnp.transpose(coefs, (1, 0, 2)).reshape(FEATS, TGT)
    residual = jnp.transpose(residuals, (1, 0, 2)).reshape(ROWS, TGT)
    return (coefficients, residual)
```

```python
import functools

import jax
import jax.numpy as jnp
from jax import lax
from jax.experimental import pallas as pl
from jax.experimental.pallas import tpu as pltpu
from jax.sharding import PartitionSpec as P

SWEEPS = 1
HI = lax.Precision.HIGHEST
GATHER_BYTES = 16 * 2**20


def shifted(block, axis, distance):
    devices = range(lax.axis_size(axis))
    route = [((i - distance) % len(devices), i) for i in devices]
    return lax.ppermute(block, axis, route)


def invert_tile(m):
    n = m.shape[0]
    lane = lax.broadcasted_iota(jnp.int32, (8, n), 1)
    sub = lax.broadcasted_iota(jnp.int32, (8, n), 0)
    lanes = lax.broadcasted_iota(jnp.int32, (n, n), 1)
    for q in range(n // 8):
        c = 8 * q
        panel = m[c : c + 8, :]
        d = [jnp.broadcast_to(panel[:, c + t : c + t + 1], (8, n)) for t in range(8)]
        mine = (lane >= c) & (lane < c + 8)
        panel = jnp.where(mine, jnp.where(lane - c == sub, 1.0, 0.0), panel)
        for t in range(8):
            inv = 1.0 / d[t][t : t + 1, :]
            row = panel[t : t + 1, :] * inv
            panel = jnp.where(sub == t, row, panel - d[t] * row)
            for u in range(t + 1, 8):
                head = d[u][t : t + 1, :] * inv
                d[u] = jnp.where(sub == t, head, d[u] - d[t] * head)
        new = jnp.where((lanes >= c) & (lanes < c + 8), 0.0, m)
        for t in range(8):
            new = new - jnp.broadcast_to(m[:, c + t : c + t + 1], (n, n)) * panel[t : t + 1, :]
        parts = [new[:c, :]] if q else []
        parts.append(panel)
        if c + 8 < n:
            parts.append(new[c + 8 :, :])
        m = jnp.concatenate(parts, axis=0)
    return m


def invert_kernel(tile, a_ref, o_ref, aside=None):
    n = a_ref.shape[0]
    o_ref[...] = a_ref[...]
    eye = jnp.where(
        lax.broadcasted_iota(jnp.int32, (tile, tile), 0)
        == lax.broadcasted_iota(jnp.int32, (tile, tile), 1),
        1.0,
        0.0,
    )

    def block(k, _):
        if aside is not None:
            pl.when(k == 1)(aside)
        at = pl.ds(pl.multiple_of(k * tile, tile), tile)
        pivot = invert_tile(o_ref[at, at])
        column = o_ref[:, at]
        o_ref[at, at] = eye
        row = jnp.dot(pivot, o_ref[at, :], precision=HI, preferred_element_type=jnp.float32)
        o_ref[:, at] = jnp.zeros((n, tile), jnp.float32)
        o_ref[...] -= jnp.dot(column, row, precision=HI, preferred_element_type=jnp.float32)
        o_ref[at, :] = row
        return 0

    lax.fori_loop(0, n // tile, block, 0)


def invert(gram):
    n = gram.shape[0]
    return pl.pallas_call(
        functools.partial(invert_kernel, min(128, n)),
        out_shape=jax.ShapeDtypeStruct((n, n), jnp.float32),
        in_specs=[pl.BlockSpec(memory_space=pltpu.VMEM)],
        out_specs=pl.BlockSpec(memory_space=pltpu.VMEM),
        cost_estimate=pl.CostEstimate(
            flops=2 * n**3 * 20, bytes_accessed=8 * n * n, transcendentals=0
        ),
    )(gram)


def tmul(a, b, precision):
    return lax.dot_general(
        a, b, (((0,), (0,)), ((), ())), precision=precision, preferred_element_type=jnp.float32
    )


def split(x):
    high = x.astype(jnp.bfloat16)
    return high, (x - high.astype(jnp.float32)).astype(jnp.bfloat16)


def dot3(a, b, contract):
    dims = (contract, ((), ()))
    mul = functools.partial(
        lax.dot_general, dimension_numbers=dims, preferred_element_type=jnp.float32
    )
    rows = a[0].shape[0]
    both = mul(jnp.concatenate(a, axis=0), b[0])
    return both[:rows] + (both[rows:] + mul(a[0], b[1]))


class RowSum:
    def __init__(self, net, k, n, src, pair_buf, rs_buf, dst):
        self.net, self.k, self.src, self.dst = net, k, src, dst
        self.pair_buf, self.rs_buf = pair_buf, rs_buf
        self.half, self.size = n // 2, n // 2 // net.nz

    def slot(self, d):
        net = self.net
        return rows_of(net.c * self.half + ((net.z + d) % net.nz) * self.size, self.size)

    def pair_slot(self, d):
        return rows_of(((self.net.z + d) % self.net.nz) * self.size, self.size)

    def swap(self):
        net = self.net
        away = self.src.at[rows_of((1 - net.c) * self.half, self.half)]
        self.sends = [net.copy(away, self.pair_buf, net.psem, (self.k,), net.mate)]
        self.sends[0].start()

    def scatter(self):
        net = self.net
        self.sends[0].wait_recv()
        for d in range(1, net.nz):
            at = self.slot(d)
            self.src[at, :] += self.pair_buf[self.pair_slot(d), :]
            copy = net.copy(
                self.src.at[at], self.rs_buf.at[d - 1], net.rsem, (self.k, d - 1), net.along(d)
            )
            copy.start()
            self.sends.append(copy)

    def finish(self, apply):
        net = self.net
        total = self.src[self.slot(0), :] + self.pair_buf[self.pair_slot(0), :]
        for d in range(1, net.nz):
            self.sends[d].wait_recv()
            total = total + self.rs_buf[d - 1]
        own = self.dst.at[self.slot(0)]
        own[...] = apply(total)
        self.spread = []
        for d in range(1, net.nz):
            copy = net.copy(own, own, net.asem, (self.k, d - 1), net.along(d))
            copy.start()
            self.spread.append(copy)
        self.relay = [net.copy(own, own, net.wsem, (self.k, 0), net.mate)]
        self.relay[0].start()

    def collect(self):
        net = self.net
        for d in range(1, net.nz):
            self.spread[d - 1].wait_recv()
            piece = self.dst.at[self.slot(net.nz - d)]
            self.relay.append(net.copy(piece, piece, net.wsem, (self.k, d), net.mate))
            self.relay[d].start()
        for copy in self.relay:
            copy.wait_recv()
        for copy in self.sends + self.spread + self.relay:
            copy.wait_send()


class Net:
    def __init__(self, nb, nrows, psem, rsem, asem, wsem):
        self.nb, self.nz = nb, nrows // 2
        self.r, self.g = lax.axis_index("rows"), lax.axis_index("feat")
        self.z, self.c = self.r // 2, self.r % 2
        self.mate = (self.r + 1 - 2 * self.c, self.g)
        self.odd = self.g % 2
        self.beside = (self.r, self.g + 1 - 2 * self.odd)
        self.across = (self.r, (self.g + 2) % 4)
        self.psem, self.rsem, self.asem, self.wsem = psem, rsem, asem, wsem

    def along(self, d):
        return (((self.z + d) % self.nz) * 2 + self.c, self.g)

    def owner_of(self, s):
        return (self.r, (self.g + s) % self.nb)

    def copy(self, src, dst, sems, at, device):
        return pltpu.make_async_remote_copy(
            src_ref=src, dst_ref=dst, send_sem=sems.at[(0,) + at], recv_sem=sems.at[(1,) + at],
            device_id=device, device_id_type=pl.DeviceIdType.MESH,
        )

    def greet(self):
        barrier = pltpu.get_barrier_semaphore()
        peers = [self.mate] + [self.along(d) for d in range(1, self.nz)]
        peers += [self.owner_of(s) for s in range(1, self.nb)]
        for peer in peers:
            pl.semaphore_signal(
                barrier, inc=1, device_id=peer, device_id_type=pl.DeviceIdType.MESH
            )
        pl.semaphore_wait(barrier, len(peers))


def rows_of(start, size):
    return pl.ds(pl.multiple_of(start, 8), size)


def tiles(count, body):
    lax.fori_loop(0, count, lambda i, _: (body(i), 0)[1], 0)


TILE = 128
CHUNKS = 2


def sweep_kernel(
    nb, nrows, x_ref, t_ref, coef_ref, out_ref,
    xbuf, xh, xl, rest, ginv, part, xt, gpart, gpair, grs, gsum, gfull, ipack, pairb, rsb, full, cbuf,
    fsem, psem, rsem, asem, wsem, isem, jsem, csem, dsem,
):
    net = Net(nb, nrows, psem, rsem, asem, wsem)
    c, g = net.c, net.g
    height, width = x_ref.shape
    tg = t_ref.shape[1]
    chunk = tg // CHUNKS
    net.greet()

    top, bottom = pl.ds(0, height // 2), pl.ds(height // 2, height // 2)
    blocks = [
        net.copy(x_ref.at[bottom], xbuf.at[0, bottom], fsem, (0,), net.beside),
        net.copy(x_ref.at[top], xbuf.at[0, top], fsem, (1,), net.beside),
        net.copy(x_ref.at[top], xbuf.at[1, top], fsem, (2,), net.across),
        net.copy(x_ref.at[bottom], xbuf.at[1, bottom], fsem, (3,), net.across),
        net.copy(xbuf.at[1, top], xbuf.at[2, top], fsem, (4,), net.beside),
        net.copy(xbuf.at[0, bottom], xbuf.at[2, bottom], fsem, (5,), net.across),
    ]

    def start_blocks(even, odd):
        @pl.when(net.odd == 0)
        def _():
            for k in even:
                blocks[k].start()

        @pl.when(net.odd == 1)
        def _():
            for k in odd:
                blocks[k].start()

    def await_blocks(even, odd):
        @pl.when(net.odd == 0)
        def _():
            for k in even:
                blocks[k].wait_recv()

        @pl.when(net.odd == 1)
        def _():
            for k in odd:
                blocks[k].wait_recv()

    def second_blocks():
        blocks[0].wait_recv()
        blocks[2].wait_recv()
        start_blocks((4, 3), (1, 5))

    def slot(s):
        if s == 2:
            return 1
        return 2 * net.odd if s == 1 else 2 - 2 * net.odd

    blocks[0].start()
    blocks[2].start()

    m = width // TILE
    pairs = [(i, j) for i in range(m) for j in range(i + 1)]
    for i in range(m):
        xt[...] = x_ref[:, i * TILE : (i + 1) * TILE].T
        low = jnp.dot(
            xt[...], x_ref[:, : (i + 1) * TILE], precision=HI, preferred_element_type=jnp.float32
        )
        for j in range(i + 1):
            at = pairs.index((i, j)) * TILE
            gpart[at : at + TILE, :] = low[:, j * TILE : (j + 1) * TILE]
    gram = RowSum(net, 0, len(pairs) * TILE, gpart, gpair, grs, gsum)
    gram.swap()

    def turn(i):
        at = pl.ds(pl.multiple_of(i * TILE, TILE), TILE)
        rest[at, :] = t_ref[:, at].T

    def cut(s):
        block = xbuf.at[slot(s)] if s else x_ref

        def body(i):
            at = pl.ds(pl.multiple_of(i * TILE, TILE), TILE)
            xh[s % 2, at, :], xl[s % 2, at, :] = split(block[at, :])

        tiles(height // TILE, body)

    sums = [
        [
            RowSum(
                net, 1 + s * CHUNKS + p, chunk, part.at[p], pairb.at[s, p], rsb.at[s, p],
                full.at[s, p],
            )
            for p in range(CHUNKS)
        ]
        for s in range(nb)
    ]

    def product(s, p):
        res = split(rest[p * chunk : (p + 1) * chunk, :])
        part[p] = dot3(res, (xh[s % 2], xl[s % 2]), ((1,), (0,)))

    def update(s, p):
        step = split(full[s, p])
        rest[p * chunk : (p + 1) * chunk, :] -= dot3(step, (xh[s % 2], xl[s % 2]), ((1,), (1,)))

    gram.scatter()
    tiles(tg // TILE, turn)
    cut(0)
    gram.finish(lambda v: v)
    for p in range(CHUNKS):
        product(0, p)
    gram.collect()
    for p in range(CHUNKS):
        sums[0][p].swap()
    for p in range(CHUNKS):
        sums[0][p].scatter()
    def unpack(packed, square):
        for at, (i, j) in enumerate(pairs):
            tile = packed[at * TILE : (at + 1) * TILE, :]
            square[i * TILE : (i + 1) * TILE, j * TILE : (j + 1) * TILE] = tile
            if i != j:
                square[j * TILE : (j + 1) * TILE, i * TILE : (i + 1) * TILE] = tile.T

    unpack(gsum, gfull)
    invert_kernel(TILE, gfull, ginv.at[0], second_blocks)
    for at, (i, j) in enumerate(pairs):
        gsum[at * TILE : (at + 1) * TILE, :] = ginv[
            0, i * TILE : (i + 1) * TILE, j * TILE : (j + 1) * TILE
        ]

    wh = width // 2
    mine = pl.ds(pl.multiple_of(c * wh, wh), wh)
    ph = len(pairs) * TILE // 2
    share = rows_of(c * ph, ph)

    def inverse_copy(s):
        return net.copy(
            gsum.at[share], ipack.at[s - 1, share], isem, (s - 1,), net.owner_of(nb - s)
        )

    def inverse_relay(s):
        piece = ipack.at[s - 1, share]
        return net.copy(piece, piece, jsem, (s - 1,), net.mate)

    for s in range(1, nb):
        inverse_copy(s).start()
    start_blocks((1, 5), (4, 3))

    def columns(group, p):
        return pl.ds(pl.multiple_of(group * tg + p * chunk, chunk), chunk)

    def coef_copy(s, p):
        return net.copy(
            cbuf.at[s - 1, p], coef_ref.at[mine, columns(g, p)], csem, (s - 1, p),
            net.owner_of(s),
        )

    def coef_relay(s, p):
        piece = coef_ref.at[mine, columns((g - s + nb) % nb, p)]
        return net.copy(piece, piece, dsem, (s - 1, p), net.mate)

    def hand_over(s, p):
        if s:
            cbuf[s - 1, p] = full[s, p, :, mine].T
            coef_copy(s, p).start()
        else:
            coef_ref[:, columns(g, p)] = full[s, p].T

    for s in range(nb):
        last = s + 1 == nb
        if s:
            inverse_relay(s).wait_recv()
            unpack(ipack.at[s - 1], ginv.at[s])
        for p in range(CHUNKS):
            sums[s][p].finish(
                lambda v: jnp.dot(v, ginv[s], precision=HI, preferred_element_type=jnp.float32)
            )
        if not last:
            inverse_copy(s + 1).wait_recv()
            inverse_relay(s + 1).start()
            await_blocks(*(((1,), (4, 5)), ((3,), (3,)), ((4, 5), (1,)))[s])
            cut(s + 1)
        for p in range(CHUNKS):
            sums[s][p].collect()
            if last:
                hand_over(s, p)
            update(s, p)
            if not last:
                product(s + 1, p)
                sums[s + 1][p].swap()
                sums[s + 1][p].scatter()
                hand_over(s, p)
        if s > 1:
            for p in range(CHUNKS):
                coef_copy(s - 1, p).wait_recv()
                coef_relay(s - 1, p).start()

    def turn_back(i):
        at = pl.ds(pl.multiple_of(i * TILE, TILE), TILE)
        out_ref[:, at] = rest[at, :].T

    tiles(tg // TILE, turn_back)
    for p in range(CHUNKS):
        coef_copy(nb - 1, p).wait_recv()
        coef_relay(nb - 1, p).start()
    for copy in blocks:
        copy.wait_send()
    for s in range(1, nb):
        for copy in (inverse_copy, inverse_relay):
            copy(s).wait_send()
        for p in range(CHUNKS):
            coef_relay(s, p).wait_recv()
            coef_copy(s, p).wait_send()
            coef_relay(s, p).wait_send()


def gathered(features, targets):
    nb, nrows = lax.axis_size("feat"), lax.axis_size("rows")
    height, width = features.shape
    tg = targets.shape[1]
    nz = nrows // 2
    chunk = tg // CHUNKS
    m = width // TILE
    packed = m * (m + 1) // 2 * TILE
    f32 = jnp.float32
    sums = 1 + nb * CHUNKS
    vmem = pl.BlockSpec(memory_space=pltpu.VMEM)
    dma = pltpu.SemaphoreType.DMA
    return pl.pallas_call(
        functools.partial(sweep_kernel, nb, nrows),
        out_shape=(
            jax.ShapeDtypeStruct((width, tg * nb), f32),
            jax.ShapeDtypeStruct((height, tg), f32),
        ),
        in_specs=[vmem] * 2,
        out_specs=(vmem, vmem),
        scratch_shapes=[
            pltpu.VMEM((nb - 1, height, width), f32),
            pltpu.VMEM((2, height, width), jnp.bfloat16),
            pltpu.VMEM((2, height, width), jnp.bfloat16),
            pltpu.VMEM((tg, height), f32),
            pltpu.VMEM((nb, width, width), f32),
            pltpu.VMEM((CHUNKS, chunk, width), f32),
            pltpu.VMEM((TILE, height), f32),
            pltpu.VMEM((packed, TILE), f32),
            pltpu.VMEM((packed // 2, TILE), f32),
            pltpu.VMEM((nz - 1, packed // nrows, TILE), f32),
            pltpu.VMEM((packed, TILE), f32),
            pltpu.VMEM((width, width), f32),
            pltpu.VMEM((nb - 1, packed, TILE), f32),
            pltpu.VMEM((nb, CHUNKS, chunk // 2, width), f32),
            pltpu.VMEM((nb, CHUNKS, nz - 1, chunk // nrows, width), f32),
            pltpu.VMEM((nb, CHUNKS, chunk, width), f32),
            pltpu.VMEM((nb - 1, CHUNKS, width // 2, chunk), f32),
            dma((2, 6)),
            dma((2, sums)),
            dma((2, sums, nz - 1)),
            dma((2, sums, nz - 1)),
            dma((2, sums, nz)),
            dma((2, nb - 1)),
            dma((2, nb - 1)),
            dma((2, nb - 1, CHUNKS)),
            dma((2, nb - 1, CHUNKS)),
        ],
        compiler_params=pltpu.CompilerParams(
            collective_id=0, has_side_effects=True, vmem_limit_bytes=58 * 2**20
        ),
    )(features, targets)


def general(features, targets):
    nblocks = lax.axis_size("feat")
    owner = lax.axis_index("feat")
    width = features.shape[1]
    group_width = targets.shape[1]
    inverse = invert(lax.psum(tmul(features, features, HI), "rows"))
    coef = jnp.zeros((width, group_width * nblocks), jnp.float32)

    def section(s, carry):
        coef, res = carry
        group = (owner - s) % nblocks
        product = tmul(features, res, HI)
        share = lax.psum_scatter(product, "rows", scatter_dimension=1, tiled=True)
        part = jnp.dot(inverse, share, precision=HI, preferred_element_type=jnp.float32)
        step = lax.all_gather(part, "rows", axis=1, tiled=True)
        start = group * group_width
        old = lax.dynamic_slice_in_dim(coef, start, group_width, 1)
        coef = lax.dynamic_update_slice_in_dim(coef, old + step, start, 1)
        res = res - jnp.dot(features, step, precision=HI, preferred_element_type=jnp.float32)
        res = shifted(res, "feat", 1)
        return (coef, res)

    return lax.fori_loop(0, SWEEPS * nblocks, section, (coef, targets))


def on_device(features, targets):
    nblocks = lax.axis_size("feat")
    nrows = lax.axis_size("rows")
    width, group_width = features.shape[1], targets.shape[1]
    fits = nblocks == 4 and nblocks * features.size * 4 <= GATHER_BYTES
    whole = nrows % 2 == 0 and nrows > 2 and features.shape[0] % 128 == 0
    packed = (width // TILE) * (width // TILE + 1) // 2 * TILE
    even = width % (2 * TILE) == 0 and packed % (8 * nrows) == 0
    even = even and group_width % (CHUNKS * max(TILE, 8 * nrows)) == 0
    if SWEEPS == 1 and fits and whole and even:
        return gathered(features, targets)
    return general(features, targets)


def solution(mesh):
    return jax.shard_map(
        on_device,
        mesh=mesh,
        in_specs=(P("rows", "feat"), P("rows", "feat")),
        out_specs=(P("feat", None), P("rows", "feat")),
        check_vma=False,
    )
```

```python
import functools

import jax
import jax.numpy as jnp
from jax import lax
from jax.experimental import pallas as pl
from jax.experimental.pallas import tpu as pltpu
from jax.sharding import PartitionSpec as P

SWEEPS = 1
HI = lax.Precision.HIGHEST
GATHER_BYTES = 16 * 2**20


def shifted(block, axis, distance):
    devices = range(lax.axis_size(axis))
    route = [((i - distance) % len(devices), i) for i in devices]
    return lax.ppermute(block, axis, route)


def invert_tile(m):
    n = m.shape[0]
    lane = lax.broadcasted_iota(jnp.int32, (8, n), 1)
    sub = lax.broadcasted_iota(jnp.int32, (8, n), 0)
    lanes = lax.broadcasted_iota(jnp.int32, (n, n), 1)
    for q in range(n // 8):
        c = 8 * q
        panel = m[c : c + 8, :]
        d = [jnp.broadcast_to(panel[:, c + t : c + t + 1], (8, n)) for t in range(8)]
        mine = (lane >= c) & (lane < c + 8)
        panel = jnp.where(mine, jnp.where(lane - c == sub, 1.0, 0.0), panel)
        for t in range(8):
            inv = 1.0 / d[t][t : t + 1, :]
            row = panel[t : t + 1, :] * inv
            panel = jnp.where(sub == t, row, panel - d[t] * row)
            for u in range(t + 1, 8):
                head = d[u][t : t + 1, :] * inv
                d[u] = jnp.where(sub == t, head, d[u] - d[t] * head)
        new = jnp.where((lanes >= c) & (lanes < c + 8), 0.0, m)
        for t in range(8):
            new = new - jnp.broadcast_to(m[:, c + t : c + t + 1], (n, n)) * panel[t : t + 1, :]
        parts = [new[:c, :]] if q else []
        parts.append(panel)
        if c + 8 < n:
            parts.append(new[c + 8 :, :])
        m = jnp.concatenate(parts, axis=0)
    return m


def invert_kernel(tile, a_ref, o_ref, aside=()):
    n = a_ref.shape[0]
    o_ref[...] = a_ref[...]
    eye = jnp.where(
        lax.broadcasted_iota(jnp.int32, (tile, tile), 0)
        == lax.broadcasted_iota(jnp.int32, (tile, tile), 1),
        1.0,
        0.0,
    )

    def block(k, _):
        for at, work in enumerate(aside):
            pl.when(k == at)(work)
        at = pl.ds(pl.multiple_of(k * tile, tile), tile)
        pivot = invert_tile(o_ref[at, at])
        column = o_ref[:, at]
        o_ref[at, at] = eye
        row = jnp.dot(pivot, o_ref[at, :], precision=HI, preferred_element_type=jnp.float32)
        o_ref[:, at] = jnp.zeros((n, tile), jnp.float32)
        o_ref[...] -= jnp.dot(column, row, precision=HI, preferred_element_type=jnp.float32)
        o_ref[at, :] = row
        return 0

    lax.fori_loop(0, n // tile, block, 0)


def invert(gram):
    n = gram.shape[0]
    return pl.pallas_call(
        functools.partial(invert_kernel, min(128, n)),
        out_shape=jax.ShapeDtypeStruct((n, n), jnp.float32),
        in_specs=[pl.BlockSpec(memory_space=pltpu.VMEM)],
        out_specs=pl.BlockSpec(memory_space=pltpu.VMEM),
        cost_estimate=pl.CostEstimate(
            flops=2 * n**3 * 20, bytes_accessed=8 * n * n, transcendentals=0
        ),
    )(gram)


def tmul(a, b, precision):
    return lax.dot_general(
        a, b, (((0,), (0,)), ((), ())), precision=precision, preferred_element_type=jnp.float32
    )


def split(x):
    high = x.astype(jnp.bfloat16)
    return high, (x - high.astype(jnp.float32)).astype(jnp.bfloat16)


def dot3(a, b, contract):
    dims = (contract, ((), ()))
    mul = functools.partial(
        lax.dot_general, dimension_numbers=dims, preferred_element_type=jnp.float32
    )
    rows = a[0].shape[0]
    both = mul(jnp.concatenate(a, axis=0), b[0])
    return both[:rows] + (both[rows:] + mul(a[0], b[1]))


class RowSum:
    def __init__(self, net, k, n, src, pair_buf, rs_buf, dst):
        self.net, self.src, self.dst = net, src, dst
        self.pair_buf, self.rs_buf = pair_buf, rs_buf
        self.half, self.size = n // 2, n // 2 // net.nz
        away = src.at[rows_of((1 - net.c) * self.half, self.half)]
        self.swapped = net.copy(away, pair_buf, net.psem, (k,), net.mate)
        if DIRECT:
            self.order = (net.skew, net.far, net.pair)
            to = [(owner, owner) for owner in self.order]
        else:
            self.order = (net.skew, net.pair, net.far)
            to = [(net.skew, net.pair), (net.pair, net.pair), (net.far, net.far)]
        self.near = [
            net.copy(src.at[self.slot(owner)], rs_buf.at[i], net.rsem, (k, i), net.up(z))
            for i, (owner, z) in enumerate(to)
        ]
        own = dst.at[self.slot(net.z)]
        self.spread = [
            net.copy(own, own, net.asem, (k, i), net.up(z))
            for i, z in enumerate((net.far, net.skew, net.pair))
        ]
        self.relay = [
            net.copy(dst.at[self.slot(z)], dst.at[self.slot(z)], net.wsem, (k, i), net.mate)
            for i, z in enumerate((net.far, net.skew, net.pair, net.z))
        ]

    def slot(self, d):
        net = self.net
        return rows_of(net.c * self.half + d * self.size, self.size)

    def pair_slot(self, d):
        return rows_of(d * self.size, self.size)

    def swap(self):
        self.swapped.start()

    def scatter(self):
        self.swapped.wait_recv()
        for i, owner in enumerate(self.order):
            self.src[self.slot(owner), :] += self.pair_buf[self.pair_slot(owner), :]
            if DIRECT or i < 2:
                self.near[i].start()

    def forward(self):
        if not DIRECT:
            self.near[0].wait_recv()
            self.src[self.slot(self.net.far), :] += self.rs_buf[0]
            self.near[2].start()

    def finish(self, apply):
        net = self.net
        total = self.src[self.slot(net.z), :] + self.pair_buf[self.pair_slot(net.z), :]
        for i in (0, 1, 2) if DIRECT else (1, 2):
            self.near[i].wait_recv()
            total = total + self.rs_buf[i]
        self.dst[self.slot(net.z), :] = apply(total)
        for copy in self.spread:
            copy.start()
        self.relay[3].start()

    def pass_on(self):
        for i in (2, 0, 1):
            self.spread[i].wait_recv()
            self.relay[i].start()

    def collect(self):
        for copy in self.relay:
            copy.wait_recv()
        for copy in [self.swapped] + self.near + self.spread + self.relay:
            copy.wait_send()


class Net:
    def __init__(self, nb, nrows, psem, rsem, asem, wsem):
        self.nb, self.nz = nb, nrows // 2
        self.r, self.g = lax.axis_index("rows"), lax.axis_index("feat")
        self.z, self.c = self.r // 2, self.r % 2
        self.pair = self.z + 1 - 2 * (self.z % 2)
        self.far, self.skew = (self.z + 2) % 4, (self.pair + 2) % 4
        self.mate = (self.r + 1 - 2 * self.c, self.g)
        self.odd = self.g % 2
        self.beside = (self.r, self.g + 1 - 2 * self.odd)
        self.across = (self.r, (self.g + 2) % 4)
        self.psem, self.rsem, self.asem, self.wsem = psem, rsem, asem, wsem

    def up(self, z):
        return (z * 2 + self.c, self.g)

    def owner_of(self, s):
        return (self.r, (self.g + s) % self.nb)

    def copy(self, src, dst, sems, at, device):
        return pltpu.make_async_remote_copy(
            src_ref=src, dst_ref=dst, send_sem=sems.at[(0,) + at], recv_sem=sems.at[(1,) + at],
            device_id=device, device_id_type=pl.DeviceIdType.MESH,
        )

    def greet(self):
        barrier = pltpu.get_barrier_semaphore()
        peers = [self.mate] + [self.up(z) for z in (self.pair, self.far, self.skew)]
        peers += [self.owner_of(s) for s in range(1, self.nb)]
        for peer in peers:
            pl.semaphore_signal(
                barrier, inc=1, device_id=peer, device_id_type=pl.DeviceIdType.MESH
            )
        pl.semaphore_wait(barrier, len(peers))


def rows_of(start, size):
    return pl.ds(pl.multiple_of(start, 8), size)


def tiles(count, body):
    lax.fori_loop(0, count, lambda i, _: (body(i), 0)[1], 0)


TILE = 128
CHUNKS = 2
DIRECT = True


def sweep_kernel(
    nb, nrows, x_ref, t_ref, coef_ref, out_ref,
    xbuf, xh, xl, rest, ginv, part, xt, gpart, gpair, grs, gsum, gfull, ipack, pairb, rsb, full, cbuf,
    fsem, psem, rsem, asem, wsem, isem, jsem, csem, dsem,
):
    net = Net(nb, nrows, psem, rsem, asem, wsem)
    c, g = net.c, net.g
    height, width = x_ref.shape
    tg = t_ref.shape[1]
    chunk = tg // CHUNKS
    net.greet()

    top, bottom = pl.ds(0, height // 2), pl.ds(height // 2, height // 2)
    blocks = [
        net.copy(x_ref.at[bottom], xbuf.at[0, bottom], fsem, (0,), net.beside),
        net.copy(x_ref.at[top], xbuf.at[0, top], fsem, (1,), net.beside),
        net.copy(x_ref.at[top], xbuf.at[1, top], fsem, (2,), net.across),
        net.copy(x_ref.at[bottom], xbuf.at[1, bottom], fsem, (3,), net.across),
        net.copy(xbuf.at[1, top], xbuf.at[2, top], fsem, (4,), net.beside),
        net.copy(xbuf.at[0, bottom], xbuf.at[2, bottom], fsem, (5,), net.across),
    ]

    def start_blocks(even, odd):
        @pl.when(net.odd == 0)
        def _():
            for k in even:
                blocks[k].start()

        @pl.when(net.odd == 1)
        def _():
            for k in odd:
                blocks[k].start()

    def await_blocks(even, odd):
        @pl.when(net.odd == 0)
        def _():
            for k in even:
                blocks[k].wait_recv()

        @pl.when(net.odd == 1)
        def _():
            for k in odd:
                blocks[k].wait_recv()

    def second_blocks():
        blocks[0].wait_recv()
        blocks[2].wait_recv()
        start_blocks((4, 3), (1, 5))

    def slot(s):
        if s == 2:
            return 1
        return 2 * net.odd if s == 1 else 2 - 2 * net.odd

    blocks[0].start()
    blocks[2].start()

    m = width // TILE
    pairs = [(i, j) for i in range(m) for j in range(i + 1)]
    for i in range(m):
        xt[...] = x_ref[:, i * TILE : (i + 1) * TILE].T
        low = jnp.dot(
            xt[...], x_ref[:, : (i + 1) * TILE], precision=HI, preferred_element_type=jnp.float32
        )
        for j in range(i + 1):
            at = pairs.index((i, j)) * TILE
            gpart[at : at + TILE, :] = low[:, j * TILE : (j + 1) * TILE]
    gram = RowSum(net, 0, len(pairs) * TILE, gpart, gpair, grs, gsum)
    gram.swap()

    def turn(i):
        at = pl.ds(pl.multiple_of(i * TILE, TILE), TILE)
        rest[at, :] = t_ref[:, at].T

    def cut(s):
        block = xbuf.at[slot(s)] if s else x_ref

        def body(i):
            at = pl.ds(pl.multiple_of(i * TILE, TILE), TILE)
            xh[s % 2, at, :], xl[s % 2, at, :] = split(block[at, :])

        tiles(height // TILE, body)

    sums = [
        [
            RowSum(
                net, 1 + s * CHUNKS + p, chunk, part.at[p], pairb.at[s, p], rsb.at[s, p],
                full.at[s, p],
            )
            for p in range(CHUNKS)
        ]
        for s in range(nb)
    ]

    def product(s, p):
        res = split(rest[p * chunk : (p + 1) * chunk, :])
        part[p] = dot3(res, (xh[s % 2], xl[s % 2]), ((1,), (0,)))

    def update(s, p):
        step = split(full[s, p])
        rest[p * chunk : (p + 1) * chunk, :] -= dot3(step, (xh[s % 2], xl[s % 2]), ((1,), (1,)))

    gram.scatter()
    tiles(tg // TILE, turn)
    gram.forward()
    cut(0)
    gram.finish(lambda v: v)
    product(0, 0)
    sums[0][0].swap()
    gram.pass_on()
    for p in range(1, CHUNKS):
        product(0, p)
        sums[0][p].swap()
    second_blocks()
    gram.collect()
    for p in range(CHUNKS):
        sums[0][p].scatter()
    def unpack(packed, square):
        for at, (i, j) in enumerate(pairs):
            tile = packed[at * TILE : (at + 1) * TILE, :]
            square[i * TILE : (i + 1) * TILE, j * TILE : (j + 1) * TILE] = tile
            if i != j:
                square[j * TILE : (j + 1) * TILE, i * TILE : (i + 1) * TILE] = tile.T

    unpack(gsum, gfull)

    def sum_ahead(work):
        def each():
            for total in sums[0]:
                work(total)

        return each

    invert_kernel(
        TILE, gfull, ginv.at[0],
        [
            lambda: None,
            sum_ahead(RowSum.forward),
            sum_ahead(lambda total: total.finish(lambda v: v)),
            sum_ahead(RowSum.pass_on),
        ],
    )
    for at, (i, j) in enumerate(pairs):
        gsum[at * TILE : (at + 1) * TILE, :] = ginv[
            0, i * TILE : (i + 1) * TILE, j * TILE : (j + 1) * TILE
        ]

    wh = width // 2
    mine = pl.ds(pl.multiple_of(c * wh, wh), wh)
    ph = len(pairs) * TILE // 2
    share = rows_of(c * ph, ph)

    def inverse_copy(s):
        return net.copy(
            gsum.at[share], ipack.at[s - 1, share], isem, (s - 1,), net.owner_of(nb - s)
        )

    def inverse_relay(s):
        piece = ipack.at[s - 1, share]
        return net.copy(piece, piece, jsem, (s - 1,), net.mate)

    inverse_copy(1).start()
    start_blocks((), (3,))
    inverse_copy(2).start()
    start_blocks((1, 5), (4,))
    inverse_copy(3).start()

    def columns(group, p):
        return pl.ds(pl.multiple_of(group * tg + p * chunk, chunk), chunk)

    def coef_copy(s, p):
        return net.copy(
            cbuf.at[s - 1, p], coef_ref.at[mine, columns(g, p)], csem, (s - 1, p),
            net.owner_of(s),
        )

    def coef_relay(s, p):
        piece = coef_ref.at[mine, columns((g - s + nb) % nb, p)]
        return net.copy(piece, piece, dsem, (s - 1, p), net.mate)

    def hand_over(s, p):
        if s:
            cbuf[s - 1, p] = full[s, p, :, mine].T
            coef_copy(s, p).start()
        else:
            coef_ref[:, columns(g, p)] = full[s, p].T

    def apply(s):
        return lambda v: jnp.dot(v, ginv[s], precision=HI, preferred_element_type=jnp.float32)

    def fetch(s):
        await_blocks(*(((1,), (4, 5)), ((3,), (3,)), ((4, 5), (1,)))[s - 1])
        cut(s)

    def ready(s):
        inverse_copy(s).wait_recv()
        inverse_relay(s).start()
        inverse_relay(s).wait_recv()
        unpack(ipack.at[s - 1], ginv.at[s])

    for total in sums[0]:
        total.collect()
    for p in range(CHUNKS):
        full[0, p] = apply(0)(full[0, p])
        update(0, p)
    fetch(1)
    for s in range(nb - 1):
        later = sums[s + 1]
        lag = 2 if DIRECT else 3
        for k in range(CHUNKS + lag):
            if k < CHUNKS and s:
                sums[s][k].pass_on()
            if 0 <= k - 1 < CHUNKS:
                later[k - 1].scatter()
            if k < CHUNKS:
                if s:
                    sums[s][k].collect()
                    update(s, k)
                product(s + 1, k)
                later[k].swap()
                hand_over(s, k)
            if 0 <= k - 2 < CHUNKS:
                later[k - 2].forward()
            if k == min(CHUNKS, lag):
                ready(s + 1)
            if k >= lag:
                later[k - lag].finish(apply(s + 1))
        if s + 2 < nb:
            fetch(s + 2)
        if s > 1:
            for p in range(CHUNKS):
                coef_copy(s - 1, p).wait_recv()
                coef_relay(s - 1, p).start()
    for p in range(CHUNKS):
        coef_copy(nb - 2, p).wait_recv()
        coef_relay(nb - 2, p).start()
    sums[nb - 1][0].pass_on()
    for p in range(CHUNKS):
        sums[nb - 1][p].collect()
        hand_over(nb - 1, p)
        if p + 1 < CHUNKS:
            sums[nb - 1][p + 1].pass_on()
        update(nb - 1, p)

    def turn_back(i):
        at = pl.ds(pl.multiple_of(i * TILE, TILE), TILE)
        out_ref[:, at] = rest[at, :].T

    tiles(tg // TILE, turn_back)
    for p in range(CHUNKS):
        coef_copy(nb - 1, p).wait_recv()
        coef_relay(nb - 1, p).start()
    for copy in blocks:
        copy.wait_send()
    for s in range(1, nb):
        for copy in (inverse_copy, inverse_relay):
            copy(s).wait_send()
        for p in range(CHUNKS):
            coef_relay(s, p).wait_recv()
            coef_copy(s, p).wait_send()
            coef_relay(s, p).wait_send()


def gathered(features, targets):
    nb, nrows = lax.axis_size("feat"), lax.axis_size("rows")
    height, width = features.shape
    tg = targets.shape[1]
    chunk = tg // CHUNKS
    m = width // TILE
    packed = m * (m + 1) // 2 * TILE
    f32 = jnp.float32
    sums = 1 + nb * CHUNKS
    vmem = pl.BlockSpec(memory_space=pltpu.VMEM)
    dma = pltpu.SemaphoreType.DMA
    return pl.pallas_call(
        functools.partial(sweep_kernel, nb, nrows),
        out_shape=(
            jax.ShapeDtypeStruct((width, tg * nb), f32),
            jax.ShapeDtypeStruct((height, tg), f32),
        ),
        in_specs=[vmem] * 2,
        out_specs=(vmem, vmem),
        scratch_shapes=[
            pltpu.VMEM((nb - 1, height, width), f32),
            pltpu.VMEM((2, height, width), jnp.bfloat16),
            pltpu.VMEM((2, height, width), jnp.bfloat16),
            pltpu.VMEM((tg, height), f32),
            pltpu.VMEM((nb, width, width), f32),
            pltpu.VMEM((CHUNKS, chunk, width), f32),
            pltpu.VMEM((TILE, height), f32),
            pltpu.VMEM((packed, TILE), f32),
            pltpu.VMEM((packed // 2, TILE), f32),
            pltpu.VMEM((3, packed // nrows, TILE), f32),
            pltpu.VMEM((packed, TILE), f32),
            pltpu.VMEM((width, width), f32),
            pltpu.VMEM((nb - 1, packed, TILE), f32),
            pltpu.VMEM((nb, CHUNKS, chunk // 2, width), f32),
            pltpu.VMEM((nb, CHUNKS, 3, chunk // nrows, width), f32),
            pltpu.VMEM((nb, CHUNKS, chunk, width), f32),
            pltpu.VMEM((nb - 1, CHUNKS, width // 2, chunk), f32),
            dma((2, 6)),
            dma((2, sums)),
            dma((2, sums, 3)),
            dma((2, sums, 3)),
            dma((2, sums, 4)),
            dma((2, nb - 1)),
            dma((2, nb - 1)),
            dma((2, nb - 1, CHUNKS)),
            dma((2, nb - 1, CHUNKS)),
        ],
        compiler_params=pltpu.CompilerParams(
            collective_id=0, has_side_effects=True, vmem_limit_bytes=58 * 2**20
        ),
    )(features, targets)


def general(features, targets):
    nblocks = lax.axis_size("feat")
    owner = lax.axis_index("feat")
    width = features.shape[1]
    group_width = targets.shape[1]
    inverse = invert(lax.psum(tmul(features, features, HI), "rows"))
    coef = jnp.zeros((width, group_width * nblocks), jnp.float32)

    def section(s, carry):
        coef, res = carry
        group = (owner - s) % nblocks
        product = tmul(features, res, HI)
        share = lax.psum_scatter(product, "rows", scatter_dimension=1, tiled=True)
        part = jnp.dot(inverse, share, precision=HI, preferred_element_type=jnp.float32)
        step = lax.all_gather(part, "rows", axis=1, tiled=True)
        start = group * group_width
        old = lax.dynamic_slice_in_dim(coef, start, group_width, 1)
        coef = lax.dynamic_update_slice_in_dim(coef, old + step, start, 1)
        res = res - jnp.dot(features, step, precision=HI, preferred_element_type=jnp.float32)
        res = shifted(res, "feat", 1)
        return (coef, res)

    return lax.fori_loop(0, SWEEPS * nblocks, section, (coef, targets))


def on_device(features, targets):
    nblocks = lax.axis_size("feat")
    nrows = lax.axis_size("rows")
    width, group_width = features.shape[1], targets.shape[1]
    fits = nblocks == 4 and nblocks * features.size * 4 <= GATHER_BYTES
    whole = nrows == 8 and features.shape[0] % 128 == 0
    packed = (width // TILE) * (width // TILE + 1) // 2 * TILE
    even = width % (2 * TILE) == 0 and packed % (8 * nrows) == 0
    even = even and group_width % (CHUNKS * max(TILE, 8 * nrows)) == 0
    if SWEEPS == 1 and fits and whole and even:
        return gathered(features, targets)
    return general(features, targets)


def solution(mesh):
    return jax.shard_map(
        on_device,
        mesh=mesh,
        in_specs=(P("rows", "feat"), P("rows", "feat")),
        out_specs=(P("feat", None), P("rows", "feat")),
        check_vma=False,
    )
```

```python
import functools

import jax
import jax.numpy as jnp
from jax import lax
from jax.experimental import pallas as pl
from jax.experimental.pallas import tpu as pltpu
from jax.sharding import PartitionSpec as P

SWEEPS = 1
HI = lax.Precision.HIGHEST
GATHER_BYTES = 16 * 2**20


def shifted(block, axis, distance):
    devices = range(lax.axis_size(axis))
    route = [((i - distance) % len(devices), i) for i in devices]
    return lax.ppermute(block, axis, route)


def invert_tile(m):
    n = m.shape[0]
    lane = lax.broadcasted_iota(jnp.int32, (8, n), 1)
    sub = lax.broadcasted_iota(jnp.int32, (8, n), 0)
    lanes = lax.broadcasted_iota(jnp.int32, (n, n), 1)
    for q in range(n // 8):
        c = 8 * q
        panel = m[c : c + 8, :]
        d = [jnp.broadcast_to(panel[:, c + t : c + t + 1], (8, n)) for t in range(8)]
        mine = (lane >= c) & (lane < c + 8)
        panel = jnp.where(mine, jnp.where(lane - c == sub, 1.0, 0.0), panel)
        for t in range(8):
            inv = 1.0 / d[t][t : t + 1, :]
            row = panel[t : t + 1, :] * inv
            panel = jnp.where(sub == t, row, panel - d[t] * row)
            for u in range(t + 1, 8):
                head = d[u][t : t + 1, :] * inv
                d[u] = jnp.where(sub == t, head, d[u] - d[t] * head)
        new = jnp.where((lanes >= c) & (lanes < c + 8), 0.0, m)
        for t in range(8):
            new = new - jnp.broadcast_to(m[:, c + t : c + t + 1], (n, n)) * panel[t : t + 1, :]
        parts = [new[:c, :]] if q else []
        parts.append(panel)
        if c + 8 < n:
            parts.append(new[c + 8 :, :])
        m = jnp.concatenate(parts, axis=0)
    return m


def invert_kernel(tile, a_ref, o_ref, aside=()):
    n = a_ref.shape[0]
    o_ref[...] = a_ref[...]
    eye = jnp.where(
        lax.broadcasted_iota(jnp.int32, (tile, tile), 0)
        == lax.broadcasted_iota(jnp.int32, (tile, tile), 1),
        1.0,
        0.0,
    )

    def block(k, _):
        for at, work in enumerate(aside):
            pl.when(k == at)(work)
        at = pl.ds(pl.multiple_of(k * tile, tile), tile)
        pivot = invert_tile(o_ref[at, at])
        column = o_ref[:, at]
        o_ref[at, at] = eye
        row = jnp.dot(pivot, o_ref[at, :], precision=HI, preferred_element_type=jnp.float32)
        o_ref[:, at] = jnp.zeros((n, tile), jnp.float32)
        o_ref[...] -= jnp.dot(column, row, precision=HI, preferred_element_type=jnp.float32)
        o_ref[at, :] = row
        return 0

    lax.fori_loop(0, n // tile, block, 0)


def invert(gram):
    n = gram.shape[0]
    return pl.pallas_call(
        functools.partial(invert_kernel, min(128, n)),
        out_shape=jax.ShapeDtypeStruct((n, n), jnp.float32),
        in_specs=[pl.BlockSpec(memory_space=pltpu.VMEM)],
        out_specs=pl.BlockSpec(memory_space=pltpu.VMEM),
        cost_estimate=pl.CostEstimate(
            flops=2 * n**3 * 20, bytes_accessed=8 * n * n, transcendentals=0
        ),
    )(gram)


def tmul(a, b, precision):
    return lax.dot_general(
        a, b, (((0,), (0,)), ((), ())), precision=precision, preferred_element_type=jnp.float32
    )


def split(x):
    high = x.astype(jnp.bfloat16)
    return high, (x - high.astype(jnp.float32)).astype(jnp.bfloat16)


def dot3(a, b, contract):
    dims = (contract, ((), ()))
    mul = functools.partial(
        lax.dot_general, dimension_numbers=dims, preferred_element_type=jnp.float32
    )
    rows = a[0].shape[0]
    both = mul(jnp.concatenate(a, axis=0), b[0])
    return both[:rows] + (both[rows:] + mul(a[0], b[1]))


class RowSum:
    def __init__(self, net, k, n, src, pair_buf, rs_buf, dst):
        self.net, self.src, self.dst = net, src, dst
        self.pair_buf, self.rs_buf = pair_buf, rs_buf
        self.half, self.size = n // 2, n // 2 // net.nz
        away = src.at[rows_of((1 - net.c) * self.half, self.half)]
        self.swapped = net.copy(away, pair_buf, net.psem, (k,), net.mate)
        if DIRECT:
            self.order = (net.skew, net.far, net.pair)
            to = [(owner, owner) for owner in self.order]
        else:
            self.order = (net.skew, net.pair, net.far)
            to = [(net.skew, net.pair), (net.pair, net.pair), (net.far, net.far)]
        self.near = [
            net.copy(src.at[self.slot(owner)], rs_buf.at[i], net.rsem, (k, i), net.up(z))
            for i, (owner, z) in enumerate(to)
        ]
        own = dst.at[self.slot(net.z)]
        self.spread = [
            net.copy(own, own, net.asem, (k, i), net.up(z))
            for i, z in enumerate((net.far, net.skew, net.pair))
        ]
        self.relay = [
            net.copy(dst.at[self.slot(z)], dst.at[self.slot(z)], net.wsem, (k, i), net.mate)
            for i, z in enumerate((net.far, net.skew, net.pair, net.z))
        ]

    def slot(self, d):
        net = self.net
        return rows_of(net.c * self.half + d * self.size, self.size)

    def pair_slot(self, d):
        return rows_of(d * self.size, self.size)

    def swap(self):
        self.swapped.start()

    def scatter(self):
        self.swapped.wait_recv()
        for i, owner in enumerate(self.order):
            self.src[self.slot(owner), :] += self.pair_buf[self.pair_slot(owner), :]
            if DIRECT or i < 2:
                self.near[i].start()

    def forward(self):
        if not DIRECT:
            self.near[0].wait_recv()
            self.src[self.slot(self.net.far), :] += self.rs_buf[0]
            self.near[2].start()

    def finish(self, apply):
        net = self.net
        total = self.src[self.slot(net.z), :] + self.pair_buf[self.pair_slot(net.z), :]
        for i in (0, 1, 2) if DIRECT else (1, 2):
            self.near[i].wait_recv()
            total = total + self.rs_buf[i]
        self.dst[self.slot(net.z), :] = apply(total)
        for copy in self.spread:
            copy.start()
        self.relay[3].start()

    def pass_on(self):
        for i in (2, 0, 1):
            self.spread[i].wait_recv()
            self.relay[i].start()

    def collect(self):
        for copy in self.relay:
            copy.wait_recv()
        for copy in [self.swapped] + self.near + self.spread + self.relay:
            copy.wait_send()


class Net:
    def __init__(self, nb, nrows, psem, rsem, asem, wsem):
        self.nb, self.nz = nb, nrows // 2
        self.r, self.g = lax.axis_index("rows"), lax.axis_index("feat")
        self.z, self.c = self.r // 2, self.r % 2
        self.pair = self.z + 1 - 2 * (self.z % 2)
        self.far, self.skew = (self.z + 2) % 4, (self.pair + 2) % 4
        self.mate = (self.r + 1 - 2 * self.c, self.g)
        self.odd = self.g % 2
        self.beside = (self.r, self.g + 1 - 2 * self.odd)
        self.across = (self.r, (self.g + 2) % 4)
        self.psem, self.rsem, self.asem, self.wsem = psem, rsem, asem, wsem

    def up(self, z):
        return (z * 2 + self.c, self.g)

    def owner_of(self, s):
        return (self.r, (self.g + s) % self.nb)

    def copy(self, src, dst, sems, at, device):
        return pltpu.make_async_remote_copy(
            src_ref=src, dst_ref=dst, send_sem=sems.at[(0,) + at], recv_sem=sems.at[(1,) + at],
            device_id=device, device_id_type=pl.DeviceIdType.MESH,
        )

    def greet(self):
        barrier = pltpu.get_barrier_semaphore()
        peers = [self.mate] + [self.up(z) for z in (self.pair, self.far, self.skew)]
        peers += [self.owner_of(s) for s in range(1, self.nb)]
        for peer in peers:
            pl.semaphore_signal(
                barrier, inc=1, device_id=peer, device_id_type=pl.DeviceIdType.MESH
            )
        pl.semaphore_wait(barrier, len(peers))


def rows_of(start, size):
    return pl.ds(pl.multiple_of(start, 8), size)


def tiles(count, body):
    lax.fori_loop(0, count, lambda i, _: (body(i), 0)[1], 0)


TILE = 128
CHUNKS = 2
DIRECT = True
FL = 2
NL = 2


def sweep_kernel(
    nb, nrows, x_ref, t_ref, coef_ref, out_ref,
    xbuf, xh, xl, rest, ginv, part, xt, gpart, gpair, grs, gsum, gfull, ipack, pairb, rsb, full, cbuf,
    fsem, psem, rsem, asem, wsem, isem, jsem, csem, dsem,
):
    net = Net(nb, nrows, psem, rsem, asem, wsem)
    c, g = net.c, net.g
    height, width = x_ref.shape
    tg = t_ref.shape[1]
    chunk = tg // CHUNKS
    net.greet()

    top, bottom = pl.ds(0, height // 2), pl.ds(height // 2, height // 2)
    blocks = [
        net.copy(x_ref.at[bottom], xbuf.at[0, bottom], fsem, (0,), net.beside),
        net.copy(x_ref.at[top], xbuf.at[0, top], fsem, (1,), net.beside),
        net.copy(x_ref.at[top], xbuf.at[1, top], fsem, (2,), net.across),
        net.copy(x_ref.at[bottom], xbuf.at[1, bottom], fsem, (3,), net.across),
        net.copy(xbuf.at[1, top], xbuf.at[2, top], fsem, (4,), net.beside),
        net.copy(xbuf.at[0, bottom], xbuf.at[2, bottom], fsem, (5,), net.across),
    ]

    def start_blocks(even, odd):
        @pl.when(net.odd == 0)
        def _():
            for k in even:
                blocks[k].start()

        @pl.when(net.odd == 1)
        def _():
            for k in odd:
                blocks[k].start()

    def await_blocks(even, odd):
        @pl.when(net.odd == 0)
        def _():
            for k in even:
                blocks[k].wait_recv()

        @pl.when(net.odd == 1)
        def _():
            for k in odd:
                blocks[k].wait_recv()

    def second_blocks():
        blocks[0].wait_recv()
        blocks[2].wait_recv()
        start_blocks((4, 3), (1, 5, 3))

    def slot(s):
        if s == 2:
            return 1
        return 2 * net.odd if s == 1 else 2 - 2 * net.odd

    blocks[0].start()
    blocks[2].start()

    m = width // TILE
    pairs = [(i, j) for i in range(m) for j in range(i + 1)]
    for i in range(m):
        xt[...] = x_ref[:, i * TILE : (i + 1) * TILE].T
        low = jnp.dot(
            xt[...], x_ref[:, : (i + 1) * TILE], precision=HI, preferred_element_type=jnp.float32
        )
        for j in range(i + 1):
            at = pairs.index((i, j)) * TILE
            gpart[at : at + TILE, :] = low[:, j * TILE : (j + 1) * TILE]
    gram = RowSum(net, 0, len(pairs) * TILE, gpart, gpair, grs, gsum)
    gram.swap()

    def turn(i):
        at = pl.ds(pl.multiple_of(i * TILE, TILE), TILE)
        rest[at, :] = t_ref[:, at].T

    def cut(s):
        block = xbuf.at[slot(s)] if s else x_ref

        def body(i):
            at = pl.ds(pl.multiple_of(i * TILE, TILE), TILE)
            xh[s % 2, at, :], xl[s % 2, at, :] = split(block[at, :])

        tiles(height // TILE, body)

    sums = [
        [
            RowSum(
                net, 1 + s * CHUNKS + p, chunk, part.at[p], pairb.at[s, p], rsb.at[s, p],
                full.at[s, p],
            )
            for p in range(CHUNKS)
        ]
        for s in range(nb)
    ]

    def product(s, p):
        res = split(rest[p * chunk : (p + 1) * chunk, :])
        part[p] = dot3(res, (xh[s % 2], xl[s % 2]), ((1,), (0,)))

    def update(s, p):
        step = split(full[s, p])
        rest[p * chunk : (p + 1) * chunk, :] -= dot3(step, (xh[s % 2], xl[s % 2]), ((1,), (1,)))

    gram.scatter()
    tiles(tg // TILE, turn)
    cut(0)
    head = CHUNKS // 2
    for p in range(head):
        product(0, p)
        sums[0][p].swap()
    gram.forward()
    sums[0][0].scatter()
    gram.finish(lambda v: v)
    for p in range(1, head):
        sums[0][p].scatter()
    for p in range(head, CHUNKS):
        product(0, p)
        sums[0][p].swap()
    gram.pass_on()
    second_blocks()
    gram.collect()
    for p in range(head, CHUNKS):
        sums[0][p].scatter()
    def unpack(packed, square):
        for at, (i, j) in enumerate(pairs):
            tile = packed[at * TILE : (at + 1) * TILE, :]
            square[i * TILE : (i + 1) * TILE, j * TILE : (j + 1) * TILE] = tile
            if i != j:
                square[j * TILE : (j + 1) * TILE, i * TILE : (i + 1) * TILE] = tile.T

    unpack(gsum, gfull)

    def finish_ahead(some):
        for total in some:
            total.forward()
        for total in some:
            total.finish(lambda v: v)

    def pass_ahead(some):
        for total in some:
            total.pass_on()

    invert_kernel(
        TILE, gfull, ginv.at[0],
        [
            lambda: None,
            lambda: finish_ahead(sums[0][:head]),
            lambda: finish_ahead(sums[0][head:]),
            lambda: pass_ahead(sums[0][:head]),
        ],
    )
    for at, (i, j) in enumerate(pairs):
        gsum[at * TILE : (at + 1) * TILE, :] = ginv[
            0, i * TILE : (i + 1) * TILE, j * TILE : (j + 1) * TILE
        ]

    wh = width // 2
    mine = pl.ds(pl.multiple_of(c * wh, wh), wh)
    ph = len(pairs) * TILE // 2
    share = rows_of(c * ph, ph)

    def inverse_copy(s):
        return net.copy(
            gsum.at[share], ipack.at[s - 1, share], isem, (s - 1,), net.owner_of(nb - s)
        )

    def inverse_relay(s):
        piece = ipack.at[s - 1, share]
        return net.copy(piece, piece, jsem, (s - 1,), net.mate)

    inverse_copy(1).start()
    inverse_copy(2).start()
    start_blocks((1, 5), (4,))
    inverse_copy(3).start()

    def columns(group, p):
        return pl.ds(pl.multiple_of(group * tg + p * chunk, chunk), chunk)

    def coef_copy(s, p):
        return net.copy(
            cbuf.at[s - 1, p], coef_ref.at[mine, columns(g, p)], csem, (s - 1, p),
            net.owner_of(s),
        )

    def coef_relay(s, p):
        piece = coef_ref.at[mine, columns((g - s + nb) % nb, p)]
        return net.copy(piece, piece, dsem, (s - 1, p), net.mate)

    def hand_over(s, p):
        if s:
            cbuf[s - 1, p] = full[s, p, :, mine].T
            coef_copy(s, p).start()
        else:
            coef_ref[:, columns(g, p)] = full[s, p].T

    def apply(s):
        return lambda v: jnp.dot(v, ginv[s], precision=HI, preferred_element_type=jnp.float32)

    def fetch(s):
        await_blocks(*(((1,), (4, 5)), ((3,), (3,)), ((4, 5), (1,)))[s - 1])
        cut(s)

    def ready(s):
        inverse_copy(s).wait_recv()
        inverse_relay(s).start()
        inverse_relay(s).wait_recv()
        unpack(ipack.at[s - 1], ginv.at[s])

    pass_ahead(sums[0][head:])
    for total in sums[0]:
        total.collect()
    for p in range(CHUNKS):
        full[0, p] = apply(0)(full[0, p])
        update(0, p)
    fetch(1)
    for s in range(nb - 1):
        later = sums[s + 1]
        for k in range(CHUNKS + NL):
            if k < CHUNKS and s:
                sums[s][k].pass_on()
            if 0 <= k - 1 < CHUNKS:
                later[k - 1].scatter()
            if k < CHUNKS:
                if s:
                    sums[s][k].collect()
                    update(s, k)
                product(s + 1, k)
                later[k].swap()
                hand_over(s, k)
            if 0 <= k - FL < CHUNKS:
                later[k - FL].forward()
            if k == NL:
                ready(s + 1)
            if k >= NL:
                later[k - NL].finish(apply(s + 1))
        if s + 2 < nb:
            fetch(s + 2)
        if s > 1:
            for p in range(CHUNKS):
                coef_copy(s - 1, p).wait_recv()
                coef_relay(s - 1, p).start()
    for p in range(CHUNKS):
        coef_copy(nb - 2, p).wait_recv()
        coef_relay(nb - 2, p).start()
    sums[nb - 1][0].pass_on()
    for p in range(CHUNKS):
        sums[nb - 1][p].collect()
        hand_over(nb - 1, p)
        if p + 1 < CHUNKS:
            sums[nb - 1][p + 1].pass_on()
        update(nb - 1, p)

    def turn_back(i):
        at = pl.ds(pl.multiple_of(i * TILE, TILE), TILE)
        out_ref[:, at] = rest[at, :].T

    tiles(tg // TILE, turn_back)
    for p in range(CHUNKS):
        coef_copy(nb - 1, p).wait_recv()
        coef_relay(nb - 1, p).start()
    for copy in blocks:
        copy.wait_send()
    for s in range(1, nb):
        for copy in (inverse_copy, inverse_relay):
            copy(s).wait_send()
        for p in range(CHUNKS):
            coef_relay(s, p).wait_recv()
            coef_copy(s, p).wait_send()
            coef_relay(s, p).wait_send()


def gathered(features, targets):
    nb, nrows = lax.axis_size("feat"), lax.axis_size("rows")
    height, width = features.shape
    tg = targets.shape[1]
    chunk = tg // CHUNKS
    m = width // TILE
    packed = m * (m + 1) // 2 * TILE
    f32 = jnp.float32
    sums = 1 + nb * CHUNKS
    vmem = pl.BlockSpec(memory_space=pltpu.VMEM)
    dma = pltpu.SemaphoreType.DMA
    return pl.pallas_call(
        functools.partial(sweep_kernel, nb, nrows),
        out_shape=(
            jax.ShapeDtypeStruct((width, tg * nb), f32),
            jax.ShapeDtypeStruct((height, tg), f32),
        ),
        in_specs=[vmem] * 2,
        out_specs=(vmem, vmem),
        scratch_shapes=[
            pltpu.VMEM((nb - 1, height, width), f32),
            pltpu.VMEM((2, height, width), jnp.bfloat16),
            pltpu.VMEM((2, height, width), jnp.bfloat16),
            pltpu.VMEM((tg, height), f32),
            pltpu.VMEM((nb, width, width), f32),
            pltpu.VMEM((CHUNKS, chunk, width), f32),
            pltpu.VMEM((TILE, height), f32),
            pltpu.VMEM((packed, TILE), f32),
            pltpu.VMEM((packed // 2, TILE), f32),
            pltpu.VMEM((3, packed // nrows, TILE), f32),
            pltpu.VMEM((packed, TILE), f32),
            pltpu.VMEM((width, width), f32),
            pltpu.VMEM((nb - 1, packed, TILE), f32),
            pltpu.VMEM((nb, CHUNKS, chunk // 2, width), f32),
            pltpu.VMEM((nb, CHUNKS, 3, chunk // nrows, width), f32),
            pltpu.VMEM((nb, CHUNKS, chunk, width), f32),
            pltpu.VMEM((nb - 1, CHUNKS, width // 2, chunk), f32),
            dma((2, 6)),
            dma((2, sums)),
            dma((2, sums, 3)),
            dma((2, sums, 3)),
            dma((2, sums, 4)),
            dma((2, nb - 1)),
            dma((2, nb - 1)),
            dma((2, nb - 1, CHUNKS)),
            dma((2, nb - 1, CHUNKS)),
        ],
        compiler_params=pltpu.CompilerParams(
            collective_id=0, has_side_effects=True, vmem_limit_bytes=58 * 2**20
        ),
    )(features, targets)


def general(features, targets):
    nblocks = lax.axis_size("feat")
    owner = lax.axis_index("feat")
    width = features.shape[1]
    group_width = targets.shape[1]
    inverse = invert(lax.psum(tmul(features, features, HI), "rows"))
    coef = jnp.zeros((width, group_width * nblocks), jnp.float32)

    def section(s, carry):
        coef, res = carry
        group = (owner - s) % nblocks
        product = tmul(features, res, HI)
        share = lax.psum_scatter(product, "rows", scatter_dimension=1, tiled=True)
        part = jnp.dot(inverse, share, precision=HI, preferred_element_type=jnp.float32)
        step = lax.all_gather(part, "rows", axis=1, tiled=True)
        start = group * group_width
        old = lax.dynamic_slice_in_dim(coef, start, group_width, 1)
        coef = lax.dynamic_update_slice_in_dim(coef, old + step, start, 1)
        res = res - jnp.dot(features, step, precision=HI, preferred_element_type=jnp.float32)
        res = shifted(res, "feat", 1)
        return (coef, res)

    return lax.fori_loop(0, SWEEPS * nblocks, section, (coef, targets))


def on_device(features, targets):
    nblocks = lax.axis_size("feat")
    nrows = lax.axis_size("rows")
    width, group_width = features.shape[1], targets.shape[1]
    fits = nblocks == 4 and nblocks * features.size * 4 <= GATHER_BYTES
    whole = nrows == 8 and features.shape[0] % 128 == 0
    packed = (width // TILE) * (width // TILE + 1) // 2 * TILE
    even = width % (2 * TILE) == 0 and packed % (8 * nrows) == 0
    even = even and group_width % (CHUNKS * max(TILE, 8 * nrows)) == 0
    if SWEEPS == 1 and fits and whole and even:
        return gathered(features, targets)
    return general(features, targets)


def solution(mesh):
    return jax.shard_map(
        on_device,
        mesh=mesh,
        in_specs=(P("rows", "feat"), P("rows", "feat")),
        out_specs=(P("feat", None), P("rows", "feat")),
        check_vma=False,
    )
```

```python
import functools

import jax
import jax.numpy as jnp
from jax import lax
from jax.experimental import pallas as pl
from jax.experimental.pallas import tpu as pltpu
from jax.sharding import PartitionSpec as P

SWEEPS = 1
HI = lax.Precision.HIGHEST
GATHER_BYTES = 16 * 2**20


def shifted(block, axis, distance):
    devices = range(lax.axis_size(axis))
    route = [((i - distance) % len(devices), i) for i in devices]
    return lax.ppermute(block, axis, route)


def invert_tile(m):
    n = m.shape[0]
    lane = lax.broadcasted_iota(jnp.int32, (8, n), 1)
    sub = lax.broadcasted_iota(jnp.int32, (8, n), 0)
    lanes = lax.broadcasted_iota(jnp.int32, (n, n), 1)
    for q in range(n // 8):
        c = 8 * q
        panel = m[c : c + 8, :]
        d = [jnp.broadcast_to(panel[:, c + t : c + t + 1], (8, n)) for t in range(8)]
        mine = (lane >= c) & (lane < c + 8)
        panel = jnp.where(mine, jnp.where(lane - c == sub, 1.0, 0.0), panel)
        for t in range(8):
            inv = 1.0 / d[t][t : t + 1, :]
            row = panel[t : t + 1, :] * inv
            panel = jnp.where(sub == t, row, panel - d[t] * row)
            for u in range(t + 1, 8):
                head = d[u][t : t + 1, :] * inv
                d[u] = jnp.where(sub == t, head, d[u] - d[t] * head)
        new = jnp.where((lanes >= c) & (lanes < c + 8), 0.0, m)
        for t in range(8):
            new = new - jnp.broadcast_to(m[:, c + t : c + t + 1], (n, n)) * panel[t : t + 1, :]
        parts = [new[:c, :]] if q else []
        parts.append(panel)
        if c + 8 < n:
            parts.append(new[c + 8 :, :])
        m = jnp.concatenate(parts, axis=0)
    return m


def invert_kernel(tile, a_ref, o_ref, aside=()):
    n = a_ref.shape[0]
    o_ref[...] = a_ref[...]
    eye = jnp.where(
        lax.broadcasted_iota(jnp.int32, (tile, tile), 0)
        == lax.broadcasted_iota(jnp.int32, (tile, tile), 1),
        1.0,
        0.0,
    )

    def block(k, _):
        for at, work in enumerate(aside):
            pl.when(k == at)(work)
        at = pl.ds(pl.multiple_of(k * tile, tile), tile)
        pivot = invert_tile(o_ref[at, at])
        column = o_ref[:, at]
        o_ref[at, at] = eye
        row = jnp.dot(pivot, o_ref[at, :], precision=HI, preferred_element_type=jnp.float32)
        o_ref[:, at] = jnp.zeros((n, tile), jnp.float32)
        o_ref[...] -= jnp.dot(column, row, precision=HI, preferred_element_type=jnp.float32)
        o_ref[at, :] = row
        return 0

    lax.fori_loop(0, n // tile, block, 0)


def invert(gram):
    n = gram.shape[0]
    return pl.pallas_call(
        functools.partial(invert_kernel, min(128, n)),
        out_shape=jax.ShapeDtypeStruct((n, n), jnp.float32),
        in_specs=[pl.BlockSpec(memory_space=pltpu.VMEM)],
        out_specs=pl.BlockSpec(memory_space=pltpu.VMEM),
        cost_estimate=pl.CostEstimate(
            flops=2 * n**3 * 20, bytes_accessed=8 * n * n, transcendentals=0
        ),
    )(gram)


def tmul(a, b, precision):
    return lax.dot_general(
        a, b, (((0,), (0,)), ((), ())), precision=precision, preferred_element_type=jnp.float32
    )


def split(x):
    high = x.astype(jnp.bfloat16)
    return high, (x - high.astype(jnp.float32)).astype(jnp.bfloat16)


def dot3(a, b, contract):
    dims = (contract, ((), ()))
    mul = functools.partial(
        lax.dot_general, dimension_numbers=dims, preferred_element_type=jnp.float32
    )
    rows = a[0].shape[0]
    both = mul(jnp.concatenate(a, axis=0), b[0])
    return both[:rows] + (both[rows:] + mul(a[0], b[1]))


class RowSum:
    def __init__(self, net, k, n, src, pair_buf, rs_buf, dst):
        self.net, self.src, self.dst = net, src, dst
        self.pair_buf, self.rs_buf = pair_buf, rs_buf
        self.half, self.size = n // 2, n // 2 // net.nz
        away = src.at[rows_of((1 - net.c) * self.half, self.half)]
        self.swapped = net.copy(away, pair_buf, net.psem, (k,), net.mate)
        if DIRECT:
            self.order = (net.skew, net.far, net.pair)
            to = [(owner, owner) for owner in self.order]
        else:
            self.order = (net.skew, net.pair, net.far)
            to = [(net.skew, net.pair), (net.pair, net.pair), (net.far, net.far)]
        self.near = [
            net.copy(src.at[self.slot(owner)], rs_buf.at[i], net.rsem, (k, i), net.up(z))
            for i, (owner, z) in enumerate(to)
        ]
        own = dst.at[self.slot(net.z)]
        self.spread = [
            net.copy(own, own, net.asem, (k, i), net.up(z))
            for i, z in enumerate((net.far, net.skew, net.pair))
        ]
        self.relay = [
            net.copy(dst.at[self.slot(z)], dst.at[self.slot(z)], net.wsem, (k, i), net.mate)
            for i, z in enumerate((net.far, net.skew, net.pair, net.z))
        ]

    def slot(self, d):
        net = self.net
        return rows_of(net.c * self.half + d * self.size, self.size)

    def pair_slot(self, d):
        return rows_of(d * self.size, self.size)

    def swap(self):
        self.swapped.start()

    def scatter(self):
        self.swapped.wait_recv()
        for i, owner in enumerate(self.order):
            self.src[self.slot(owner), :] += self.pair_buf[self.pair_slot(owner), :]
            if DIRECT or i < 2:
                self.near[i].start()

    def forward(self):
        if not DIRECT:
            self.near[0].wait_recv()
            self.src[self.slot(self.net.far), :] += self.rs_buf[0]
            self.near[2].start()

    def finish(self, apply):
        net = self.net
        total = self.src[self.slot(net.z), :] + self.pair_buf[self.pair_slot(net.z), :]
        for i in (0, 1, 2) if DIRECT else (1, 2):
            self.near[i].wait_recv()
            total = total + self.rs_buf[i]
        self.dst[self.slot(net.z), :] = apply(total)
        for copy in self.spread:
            copy.start()
        self.relay[3].start()

    def pass_on(self):
        for i in (2, 0, 1):
            self.spread[i].wait_recv()
            self.relay[i].start()

    def collect(self):
        for copy in self.relay:
            copy.wait_recv()
        for copy in [self.swapped] + self.near:
            copy.wait_send()

    def settle(self):
        for copy in self.spread + self.relay:
            copy.wait_send()


class Net:
    def __init__(self, nb, nrows, psem, rsem, asem, wsem):
        self.nb, self.nz = nb, nrows // 2
        self.r, self.g = lax.axis_index("rows"), lax.axis_index("feat")
        self.z, self.c = self.r // 2, self.r % 2
        self.pair = self.z + 1 - 2 * (self.z % 2)
        self.far, self.skew = (self.z + 2) % 4, (self.pair + 2) % 4
        self.mate = (self.r + 1 - 2 * self.c, self.g)
        self.odd = self.g % 2
        self.beside = (self.r, self.g + 1 - 2 * self.odd)
        self.across = (self.r, (self.g + 2) % 4)
        self.psem, self.rsem, self.asem, self.wsem = psem, rsem, asem, wsem

    def up(self, z):
        return (z * 2 + self.c, self.g)

    def owner_of(self, s):
        return (self.r, (self.g + s) % self.nb)

    def copy(self, src, dst, sems, at, device):
        return pltpu.make_async_remote_copy(
            src_ref=src, dst_ref=dst, send_sem=sems.at[(0,) + at], recv_sem=sems.at[(1,) + at],
            device_id=device, device_id_type=pl.DeviceIdType.MESH,
        )

    def greet(self):
        barrier = pltpu.get_barrier_semaphore()
        peers = [self.mate] + [self.up(z) for z in (self.pair, self.far, self.skew)]
        peers += [self.owner_of(s) for s in range(1, self.nb)]
        for peer in peers:
            pl.semaphore_signal(
                barrier, inc=1, device_id=peer, device_id_type=pl.DeviceIdType.MESH
            )
        pl.semaphore_wait(barrier, len(peers))


def rows_of(start, size):
    return pl.ds(pl.multiple_of(start, 8), size)


def tiles(count, body):
    lax.fori_loop(0, count, lambda i, _: (body(i), 0)[1], 0)


TILE = 128
CHUNKS = 2
DIRECT = True
FL = 2
NL = 2


def sweep_kernel(
    nb, nrows, x_ref, t_ref, coef_ref, out_ref,
    xbuf, xh, xl, rest, ginv, part, xt, gpart, gpair, grs, gsum, gfull, ipack, pairb, rsb, full, cbuf, landed,
    fsem, psem, rsem, asem, wsem, isem, jsem, csem, dsem,
):
    net = Net(nb, nrows, psem, rsem, asem, wsem)
    c, g = net.c, net.g
    height, width = x_ref.shape
    tg = t_ref.shape[1]
    chunk = tg // CHUNKS
    net.greet()

    top, bottom = pl.ds(0, height // 2), pl.ds(height // 2, height // 2)
    blocks = [
        net.copy(x_ref.at[bottom], xbuf.at[0, bottom], fsem, (0,), net.beside),
        net.copy(x_ref.at[top], xbuf.at[0, top], fsem, (1,), net.beside),
        net.copy(x_ref.at[top], xbuf.at[1, top], fsem, (2,), net.across),
        net.copy(x_ref.at[bottom], xbuf.at[1, bottom], fsem, (3,), net.across),
        net.copy(xbuf.at[1, top], xbuf.at[2, top], fsem, (4,), net.beside),
        net.copy(xbuf.at[0, bottom], xbuf.at[2, bottom], fsem, (5,), net.across),
    ]

    def start_blocks(even, odd):
        @pl.when(net.odd == 0)
        def _():
            for k in even:
                blocks[k].start()

        @pl.when(net.odd == 1)
        def _():
            for k in odd:
                blocks[k].start()

    def await_blocks(even, odd):
        @pl.when(net.odd == 0)
        def _():
            for k in even:
                blocks[k].wait_recv()

        @pl.when(net.odd == 1)
        def _():
            for k in odd:
                blocks[k].wait_recv()

    def second_blocks():
        blocks[0].wait_recv()
        blocks[2].wait_recv()
        start_blocks((4, 3), (1, 5, 3))

    def slot(s):
        if s == 2:
            return 1
        return 2 * net.odd if s == 1 else 2 - 2 * net.odd

    blocks[0].start()
    blocks[2].start()

    m = width // TILE
    pairs = [(i, j) for i in range(m) for j in range(i + 1)]
    for i in range(m):
        xt[...] = x_ref[:, i * TILE : (i + 1) * TILE].T
        low = jnp.dot(
            xt[...], x_ref[:, : (i + 1) * TILE], precision=HI, preferred_element_type=jnp.float32
        )
        for j in range(i + 1):
            at = pairs.index((i, j)) * TILE
            gpart[at : at + TILE, :] = low[:, j * TILE : (j + 1) * TILE]
    gram = RowSum(net, 0, len(pairs) * TILE, gpart, gpair, grs, gsum)
    gram.swap()

    def turn(i):
        at = pl.ds(pl.multiple_of(i * TILE, TILE), TILE)
        rest[at, :] = t_ref[:, at].T

    def cut(s):
        block = xbuf.at[slot(s)] if s else x_ref

        def body(i):
            at = pl.ds(pl.multiple_of(i * TILE, TILE), TILE)
            xh[s % 2, at, :], xl[s % 2, at, :] = split(block[at, :])

        tiles(height // TILE, body)

    sums = [
        [
            RowSum(
                net, 1 + s * CHUNKS + p, chunk, part.at[p], pairb.at[s, p], rsb.at[s, p],
                full.at[s, p],
            )
            for p in range(CHUNKS)
        ]
        for s in range(nb)
    ]

    def product(s, p):
        res = split(rest[p * chunk : (p + 1) * chunk, :])
        part[p] = dot3(res, (xh[s % 2], xl[s % 2]), ((1,), (0,)))

    def update(s, p):
        step = split(full[s, p])
        rest[p * chunk : (p + 1) * chunk, :] -= dot3(step, (xh[s % 2], xl[s % 2]), ((1,), (1,)))

    gram.scatter()
    tiles(tg // TILE, turn)
    cut(0)
    head = CHUNKS // 2
    for p in range(head):
        product(0, p)
        sums[0][p].swap()
    gram.forward()
    sums[0][0].scatter()
    gram.finish(lambda v: v)
    for p in range(1, head):
        sums[0][p].scatter()
    for p in range(head, CHUNKS):
        product(0, p)
        sums[0][p].swap()
    gram.pass_on()
    second_blocks()
    gram.collect()
    gram.settle()
    for p in range(head, CHUNKS):
        sums[0][p].scatter()
    def unpack(packed, square):
        for at, (i, j) in enumerate(pairs):
            tile = packed[at * TILE : (at + 1) * TILE, :]
            square[i * TILE : (i + 1) * TILE, j * TILE : (j + 1) * TILE] = tile
            if i != j:
                square[j * TILE : (j + 1) * TILE, i * TILE : (i + 1) * TILE] = tile.T

    unpack(gsum, gfull)

    def finish_ahead(some):
        for total in some:
            total.forward()
        for total in some:
            total.finish(lambda v: v)

    def pass_ahead(some):
        for total in some:
            total.pass_on()

    invert_kernel(
        TILE, gfull, ginv.at[0],
        [
            lambda: None,
            lambda: finish_ahead(sums[0][:head]),
            lambda: finish_ahead(sums[0][head:]),
            lambda: pass_ahead(sums[0][:head]),
        ],
    )
    for at, (i, j) in enumerate(pairs):
        gsum[at * TILE : (at + 1) * TILE, :] = ginv[
            0, i * TILE : (i + 1) * TILE, j * TILE : (j + 1) * TILE
        ]

    wh = width // 2
    mine = pl.ds(pl.multiple_of(c * wh, wh), wh)
    ph = len(pairs) * TILE // 2
    share = rows_of(c * ph, ph)

    def inverse_copy(s):
        return net.copy(
            gsum.at[share], ipack.at[s - 1, share], isem, (s - 1,), net.owner_of(nb - s)
        )

    def inverse_relay(s):
        piece = ipack.at[s - 1, share]
        return net.copy(piece, piece, jsem, (s - 1,), net.mate)

    inverse_copy(1).start()
    inverse_copy(2).start()
    start_blocks((1, 5), (4,))
    inverse_copy(3).start()

    def columns(group, p):
        return pl.ds(pl.multiple_of(group * tg + p * chunk, chunk), chunk)

    def coef_copy(s, p):
        return net.copy(
            cbuf.at[s - 1, p], landed.at[s - 1, p, mine], csem, (s - 1, p),
            net.owner_of(s),
        )

    def coef_relay(s, p):
        piece = landed.at[s - 1, p, mine]
        return net.copy(piece, piece, dsem, (s - 1, p), net.mate)

    def hand_over(s, p):
        if s:
            cbuf[s - 1, p] = full[s, p, :, mine].T
            coef_copy(s, p).start()
        else:
            coef_ref[:, columns(g, p)] = full[s, p].T

    def apply(s):
        return lambda v: jnp.dot(v, ginv[s], precision=HI, preferred_element_type=jnp.float32)

    def fetch(s):
        await_blocks(*(((1,), (4, 5)), ((3,), (3,)), ((4, 5), (1,)))[s - 1])
        cut(s)

    def ready(s):
        inverse_copy(s).wait_recv()
        inverse_relay(s).start()
        inverse_relay(s).wait_recv()
        unpack(ipack.at[s - 1], ginv.at[s])

    pass_ahead(sums[0][head:])
    for total in sums[0]:
        total.collect()
        total.settle()
    for p in range(CHUNKS):
        full[0, p] = apply(0)(full[0, p])
        update(0, p)
    fetch(1)
    for s in range(nb - 1):
        later = sums[s + 1]
        for k in range(CHUNKS + NL):
            if k < CHUNKS and s:
                sums[s][k].pass_on()
            if 0 <= k - 1 < CHUNKS:
                later[k - 1].scatter()
            if k < CHUNKS:
                if s:
                    sums[s][k].collect()
                    update(s, k)
                product(s + 1, k)
                later[k].swap()
            if 0 <= k - 1 < CHUNKS:
                hand_over(s, k - 1)
            if 0 <= k - FL < CHUNKS:
                later[k - FL].forward()
            if k == NL:
                ready(s + 1)
            if k >= NL:
                later[k - NL].finish(apply(s + 1))
        if s + 2 < nb:
            fetch(s + 2)
        if s > 1:
            for p in range(CHUNKS):
                coef_copy(s - 1, p).wait_recv()
                coef_relay(s - 1, p).start()
    for p in range(CHUNKS):
        coef_copy(nb - 2, p).wait_recv()
        coef_relay(nb - 2, p).start()
    sums[nb - 1][0].pass_on()
    for p in range(CHUNKS):
        sums[nb - 1][p].collect()
        hand_over(nb - 1, p)
        if p + 1 < CHUNKS:
            sums[nb - 1][p + 1].pass_on()
        update(nb - 1, p)

    def turn_back(i):
        at = pl.ds(pl.multiple_of(i * TILE, TILE), TILE)
        out_ref[:, at] = rest[at, :].T

    tiles(tg // TILE, turn_back)
    for p in range(CHUNKS):
        coef_copy(nb - 1, p).wait_recv()
        coef_relay(nb - 1, p).start()
    for copy in blocks:
        copy.wait_send()
    for s in range(1, nb):
        for total in sums[s]:
            total.settle()
    for s in range(1, nb):
        for copy in (inverse_copy, inverse_relay):
            copy(s).wait_send()
        for p in range(CHUNKS):
            coef_relay(s, p).wait_recv()
            coef_ref[:, columns((g - s + nb) % nb, p)] = landed[s - 1, p]
            coef_copy(s, p).wait_send()
            coef_relay(s, p).wait_send()


def gathered(features, targets):
    nb, nrows = lax.axis_size("feat"), lax.axis_size("rows")
    height, width = features.shape
    tg = targets.shape[1]
    chunk = tg // CHUNKS
    m = width // TILE
    packed = m * (m + 1) // 2 * TILE
    f32 = jnp.float32
    sums = 1 + nb * CHUNKS
    vmem = pl.BlockSpec(memory_space=pltpu.VMEM)
    dma = pltpu.SemaphoreType.DMA
    return pl.pallas_call(
        functools.partial(sweep_kernel, nb, nrows),
        out_shape=(
            jax.ShapeDtypeStruct((width, tg * nb), f32),
            jax.ShapeDtypeStruct((height, tg), f32),
        ),
        in_specs=[vmem] * 2,
        out_specs=(vmem, vmem),
        scratch_shapes=[
            pltpu.VMEM((nb - 1, height, width), f32),
            pltpu.VMEM((2, height, width), jnp.bfloat16),
            pltpu.VMEM((2, height, width), jnp.bfloat16),
            pltpu.VMEM((tg, height), f32),
            pltpu.VMEM((nb, width, width), f32),
            pltpu.VMEM((CHUNKS, chunk, width), f32),
            pltpu.VMEM((TILE, height), f32),
            pltpu.VMEM((packed, TILE), f32),
            pltpu.VMEM((packed // 2, TILE), f32),
            pltpu.VMEM((3, packed // nrows, TILE), f32),
            pltpu.VMEM((packed, TILE), f32),
            pltpu.VMEM((width, width), f32),
            pltpu.VMEM((nb - 1, packed, TILE), f32),
            pltpu.VMEM((nb, CHUNKS, chunk // 2, width), f32),
            pltpu.VMEM((nb, CHUNKS, 3, chunk // nrows, width), f32),
            pltpu.VMEM((nb, CHUNKS, chunk, width), f32),
            pltpu.VMEM((nb - 1, CHUNKS, width // 2, chunk), f32),
            pltpu.VMEM((nb - 1, CHUNKS, width, chunk), f32),
            dma((2, 6)),
            dma((2, sums)),
            dma((2, sums, 3)),
            dma((2, sums, 3)),
            dma((2, sums, 4)),
            dma((2, nb - 1)),
            dma((2, nb - 1)),
            dma((2, nb - 1, CHUNKS)),
            dma((2, nb - 1, CHUNKS)),
        ],
        compiler_params=pltpu.CompilerParams(
            collective_id=0, has_side_effects=True, vmem_limit_bytes=58 * 2**20
        ),
    )(features, targets)


def general(features, targets):
    nblocks = lax.axis_size("feat")
    owner = lax.axis_index("feat")
    width = features.shape[1]
    group_width = targets.shape[1]
    inverse = invert(lax.psum(tmul(features, features, HI), "rows"))
    coef = jnp.zeros((width, group_width * nblocks), jnp.float32)

    def section(s, carry):
        coef, res = carry
        group = (owner - s) % nblocks
        product = tmul(features, res, HI)
        share = lax.psum_scatter(product, "rows", scatter_dimension=1, tiled=True)
        part = jnp.dot(inverse, share, precision=HI, preferred_element_type=jnp.float32)
        step = lax.all_gather(part, "rows", axis=1, tiled=True)
        start = group * group_width
        old = lax.dynamic_slice_in_dim(coef, start, group_width, 1)
        coef = lax.dynamic_update_slice_in_dim(coef, old + step, start, 1)
        res = res - jnp.dot(features, step, precision=HI, preferred_element_type=jnp.float32)
        res = shifted(res, "feat", 1)
        return (coef, res)

    return lax.fori_loop(0, SWEEPS * nblocks, section, (coef, targets))


def on_device(features, targets):
    nblocks = lax.axis_size("feat")
    nrows = lax.axis_size("rows")
    width, group_width = features.shape[1], targets.shape[1]
    fits = nblocks == 4 and nblocks * features.size * 4 <= GATHER_BYTES
    whole = nrows == 8 and features.shape[0] % 128 == 0
    packed = (width // TILE) * (width // TILE + 1) // 2 * TILE
    even = width % (2 * TILE) == 0 and packed % (8 * nrows) == 0
    even = even and group_width % (CHUNKS * max(TILE, 8 * nrows)) == 0
    if SWEEPS == 1 and fits and whole and even:
        return gathered(features, targets)
    return general(features, targets)


def solution(mesh):
    return jax.shard_map(
        on_device,
        mesh=mesh,
        in_specs=(P("rows", "feat"), P("rows", "feat")),
        out_specs=(P("feat", None), P("rows", "feat")),
        check_vma=False,
    )
```
